512 devices in a mesh: row: 16 (over x, y), col: 32 (over z, core).
Axes of the slice: x: 4, y: 4, z: 16, core: 2. Of those that a mesh axis runs over, the one named last changes fastest.
Arguments:
- l_rows: float32 [4096, 16384], P('row', 'col'), may hold values from -6 to 6
- v_prev: float32 [16384, 1024], P('col', 'row'), may hold values from -0.046875 to 0.046875
- l_tail: float32 [4096, 4096], P('row', 'col'), may hold values from -5 to 100, as said below
- k_cross: float32 [4096, 1024], P('row', 'col'), may hold values from -6 to 6
- k_query: float32 [1024, 1024], P('row', 'col'), may hold values from -2 to 5, as said below
Outputs:
- tail_solution: float32 [4096, 1024], P('row', 'col')
- posterior: float32 [1024, 1024], P('row', 'col')
The draws below stay inside these ranges and needn't reach their ends.
Inputs may be any that keep to these rules, and one draw needn't show every extreme that they name: `l_tail`: lower triangular; its diagonal lies between 40 and 100. `k_query`: symmetric.
All inputs are finite; a program needn't handle non-finite values.
Results may differ from the reference program's by a relative error of at most 0.000076.
Values sent between devices are 32-bit elements; how exact they have to be, the bound alone decides.
No kernel may reach another device: no remote copies, remote signals or barrier semaphores. Data moves between devices by JAX's collectives and lax.ppermute only.
A program may use at most 64 MiB of HBM per device.

```python
import math
import jax
import jax.numpy as jnp
from jax import lax

PANEL = 2048
Q = 1024
M = 16384
TAIL = 4096


def draw_l_tail(key, part):
    order = 2 * PANEL
    key_off, key_diag = jax.random.split(jax.random.fold_in(key, 11))
    lower = jnp.clip(1.5 * jax.random.normal(key_off, (order, order), jnp.float32), -5.0, 5.0)
    scales = jnp.exp(jax.random.uniform(key_diag, (order,), jnp.float32, math.log(40.0), math.log(100.0)))
    return jnp.tril(lower, -1) + jnp.diag(scales)


def draw_k_query(key, part):
    key_base = jax.random.fold_in(key, 23)
    spread = 0.3 * jax.random.normal(key_base, (Q, Q), jnp.float32)
    return 0.5 * (spread + spread.T) + 3.0 * jnp.eye(Q, dtype=jnp.float32)


def level_of(stream_key, extent, cuts, smallest, high):
    level, own = 1.0, jax.random.fold_in(stream_key, 6)
    for position, blocks in cuts:
        draws = jnp.exp(jax.random.uniform(jax.random.fold_in(own, position), (blocks,), jnp.float32, smallest / len(cuts), high / len(cuts)))
        level = level * jnp.repeat(draws, extent[position] // blocks).reshape([-1 if axis == position else 1 for axis in range(len(extent))])
    return level


def normal_values(own_key, extent, deviation, reach, shards=(), kind=jnp.bfloat16):
    result = jax.random.normal(own_key, extent, jnp.float32) * deviation
    if len(shards) > 0:
        result = level_of(own_key, extent, shards, -0.22, 0.18) * result
    return jnp.clip(result, min=-reach, max=reach).astype(kind)


def setup_inputs(seed: int = 0) -> dict:
    key_of = jax.random.split(jax.random.key(seed), 6)
    return {
        "l_rows": normal_values(key_of[0], (TAIL, M), 1.0, 6.0, ((0, 16), (1, 32)), jnp.float32),
        "v_prev": normal_values(key_of[1], (M, Q), M ** -0.5, 0.046875, ((0, 32), (1, 16)), jnp.float32),
        "l_tail": draw_l_tail(jax.random.fold_in(key_of[5], 71), 0),
        "k_cross": normal_values(key_of[3], (TAIL, Q), 1.0, 6.0, ((0, 16), (1, 32)), jnp.float32),
        "k_query": draw_k_query(jax.random.fold_in(key_of[5], 71), 0),
    }


def reference(l_rows, v_prev, l_tail, k_cross, k_query):
    highest = lax.Precision.HIGHEST
    residual = k_cross - jnp.dot(l_rows.astype(jnp.float32), v_prev.astype(jnp.float32), precision=highest, preferred_element_type=jnp.float32)
    tail_solution = jax.scipy.linalg.solve_triangular(l_tail, residual, lower=True)
    gram = jnp.dot(v_prev.T.astype(jnp.float32), v_prev.astype(jnp.float32), precision=highest, preferred_element_type=jnp.float32)
    gram = gram + jnp.dot(tail_solution.T.astype(jnp.float32), tail_solution.astype(jnp.float32), precision=highest, preferred_element_type=jnp.float32)
    return (tail_solution, k_query - gram)
```

```python
import functools
import jax
import jax.numpy as jnp
from jax import lax
from jax.experimental import pallas as pl
from jax.experimental.pallas import tpu as pltpu
from jax.sharding import Mesh, PartitionSpec as P

HI = lax.Precision.HIGHEST
PLANE = ("x", "y")
PLANE_T = ("y", "x")


def contract(a, b, dims):
    return lax.dot_general(a, b, (dims, ((), ())), precision=HI, preferred_element_type=jnp.float32)


def share(value, axis, count):
    return lax.all_to_all(jnp.broadcast_to(value[None], (count,) + value.shape), axis, 0, 0)


def swap(value):
    return lax.ppermute(value, "k", [(0, 1), (1, 0)])


def invert_kernel(d_ref, o_ref):
    d = d_ref[...]
    n = d.shape[0]
    row = lax.broadcasted_iota(jnp.int32, (n, n), 0)
    col = lax.broadcasted_iota(jnp.int32, (n, n), 1)
    x = jnp.where(row == col, 1.0 / d, 0.0)
    b = 1
    while b < n:
        same = (row // (2 * b)) == (col // (2 * b))
        below = same & ((row // b) % 2 == 1) & ((col // b) % 2 == 0)
        off = jnp.where(below, d, 0.0)
        t = jnp.dot(x, off, precision=HI, preferred_element_type=jnp.float32)
        x = x - jnp.dot(t, x, precision=HI, preferred_element_type=jnp.float32)
        b *= 2
    o_ref[...] = x


def invert(d):
    return pl.pallas_call(
        invert_kernel,
        out_shape=jax.ShapeDtypeStruct(d.shape, jnp.float32),
        in_specs=[pl.BlockSpec(memory_space=pltpu.VMEM)],
        out_specs=pl.BlockSpec(memory_space=pltpu.VMEM),
        name="invert_block",
    )(d)


def body(l_rows, v_prev, l_tail, k_cross, k_query):
    x_id, y_id, k_id = lax.axis_index("x"), lax.axis_index("y"), lax.axis_index("k")
    rows = l_rows.shape[0]
    qc = k_cross.shape[1]

    with jax.named_scope("gather_l"):
        panels = lax.all_gather(l_tail, ("zh", "zl", "k"), axis=0)

    with jax.named_scope("stage1"):
        vt = v_prev.T
        vt_other = swap(vt)
        l_other = swap(l_rows)
        v_pair = jnp.concatenate([vt, vt_other], axis=1)
        l_pair = jnp.concatenate([l_rows, l_other], axis=1)
        v_half = lax.dynamic_slice_in_dim(v_pair, k_id * qc, qc, 0)
        v_all = share(v_half, PLANE_T, 16)
        update = contract(v_all, l_pair, ((2,), (1,)))
        prior = contract(v_all, v_pair, ((2,), (1,)))
    with jax.named_scope("reduce_z"):
        both = jnp.concatenate([update, prior], axis=2).reshape(4, 4, qc, -1)
        both = lax.all_to_all(both, "zl", 0, 0).sum(0)
        both = lax.all_to_all(both, "zh", 0, 0).sum(0)
        rest = k_cross.T - both[:, :rows]
        gram_prior = both[:, rows:]

    with jax.named_scope("inverse"):
        factor = panels.transpose(1, 0, 2).reshape(rows, -1)
        own = lax.dynamic_slice_in_dim(factor, x_id * 4 * rows, 4 * rows, 1)
        diag = invert(lax.dynamic_slice_in_dim(own, y_id * rows, rows, 1))
        sent = jnp.concatenate([own[:, : 3 * rows], diag], axis=1)
        group = share(sent, "y", 4)
        zero = jnp.zeros_like(diag)
        inv = [None] * 4
        for m in (3, 2, 1, 0):
            if m < 3:
                left = jnp.concatenate(inv[m + 1 :], axis=1)
                right = group[m + 1 :, :, m * rows : (m + 1) * rows].reshape(-1, rows)
                t = contract(left, right, ((1,), (0,)))
                t = contract(t, group[m, :, 3 * rows :], ((1,), (0,)))
                inv[m] = jnp.where(m == y_id, diag, jnp.where(m < y_id, -t, zero))
            else:
                inv[m] = jnp.where(m == y_id, diag, zero)
        inverse = jnp.concatenate(inv, axis=1)

    solved = jnp.zeros_like(rest)
    for j in range(4):
        with jax.named_scope(f"solve{j}"):
            right = share(rest, "y", 4).transpose(1, 0, 2).reshape(qc, -1)
            mine = contract(right, inverse, ((1,), (1,)))
            solved = jnp.where(x_id == j, mine, solved)
            if j < 3:
                known = share(solved, PLANE, 16)[4 * j : 4 * j + 4]
                known = known.transpose(1, 0, 2).reshape(qc, -1)
                rest = rest - contract(known, factor[:, j * 4 * rows : (j + 1) * 4 * rows], ((1,), (1,)))

    with jax.named_scope("gram"):
        near = share(solved, "zh", 4)
        near = share(near, "zl", 4)
        far = swap(near)
        ga = contract(near, solved, ((3,), (1,)))
        gb = contract(far, solved, ((3,), (1,)))
        first = jnp.where(k_id == 0, ga, gb)
        second = jnp.where(k_id == 0, gb, ga)
        part = jnp.concatenate([first, second], axis=2).reshape(16, 2 * qc, qc)
        gram_tail = lax.all_to_all(part, PLANE_T, 0, 0).sum(0)
        posterior = k_query - (gram_prior.T + gram_tail)
    return solved.T, posterior


def solution(mesh):
    fine = Mesh(mesh.devices.reshape(4, 4, 4, 4, 2), ("x", "y", "zh", "zl", "k"))
    row, col = ("x", "y"), ("zh", "zl", "k")
    in_specs = (P(row, col), P(col, row), P(row, col), P(row, col), P(row, col))
    return jax.shard_map(body, mesh=fine, in_specs=in_specs, out_specs=(P(row, col), P(row, col)), check_vma=False)
```

```python
import functools
import jax
import jax.numpy as jnp
from jax import lax
from jax.experimental import pallas as pl
from jax.experimental.pallas import tpu as pltpu
from jax.sharding import Mesh, PartitionSpec as P

HI = lax.Precision.HIGHEST
PLANE_T = ("y", "x")
GRANT = 16 * 1024 * 1024
VMEM = pl.BlockSpec(memory_space=pltpu.VMEM)


def contract(a, b, dims):
    return lax.dot_general(a, b, (dims, ((), ())), precision=HI, preferred_element_type=jnp.float32)


def mul(a, b):
    return jnp.dot(a, b, precision=HI, preferred_element_type=jnp.float32)


def share(value, axis, count):
    return lax.all_to_all(jnp.broadcast_to(value[None], (count,) + value.shape), axis, 0, 0)


def swap(value):
    return lax.ppermute(value, "k", [(0, 1), (1, 0)])


def f32(*shape):
    return jax.ShapeDtypeStruct(shape, jnp.float32)


def local(kernel, out_shape, name, *operands, flops=0):
    outs = out_shape if isinstance(out_shape, tuple) else (out_shape,)
    moved = sum(4 * o.size for o in operands) + sum(4 * o.size for o in outs)
    return pl.pallas_call(
        kernel,
        out_shape=out_shape,
        in_specs=[VMEM] * len(operands),
        out_specs=tuple(VMEM for _ in outs) if isinstance(out_shape, tuple) else VMEM,
        cost_estimate=pl.CostEstimate(flops=flops, bytes_accessed=moved, transcendentals=0),
        compiler_params=pltpu.CompilerParams(vmem_limit_bytes=GRANT),
        name=name,
    )(*operands)


def invert_kernel(own_ref, other_ref, o_ref, full):
    first = lax.axis_index("k") == 0
    a, b = own_ref[...], other_ref[...]
    u = jnp.concatenate([jnp.where(first, a, b), jnp.where(first, b, a)], axis=0)
    n = u.shape[0]
    row = lax.broadcasted_iota(jnp.int32, (n, n), 0)
    col = lax.broadcasted_iota(jnp.int32, (n, n), 1)
    x = jnp.where(row == col, 1.0 / u, 0.0)
    s = 0
    while (1 << s) < n:
        above = ((row >> (s + 1)) == (col >> (s + 1))) & (((row >> s) & 1) == 0) & (((col >> s) & 1) == 1)
        x = x - mul(mul(x, jnp.where(above, u, 0.0)), x)
        s += 1
    full[...] = x
    half = o_ref.shape[0]
    o_ref[...] = full[pl.ds(pl.multiple_of(lax.axis_index("k") * half, half), half), :]


def invert(own, other):
    half, n = own.shape
    return pl.pallas_call(
        invert_kernel,
        out_shape=f32(half, n),
        in_specs=[VMEM, VMEM],
        out_specs=VMEM,
        scratch_shapes=[pltpu.VMEM((n, n), jnp.float32)],
        cost_estimate=pl.CostEstimate(flops=32 * 6 * n * n * n, bytes_accessed=12 * half * n, transcendentals=0),
        compiler_params=pltpu.CompilerParams(vmem_limit_bytes=GRANT),
        name="invert_block",
    )(own, other)


def pack_kernel(own_ref, o_ref):
    half = o_ref.shape[1]
    rows = pl.ds(pl.multiple_of(lax.axis_index("k") * half, half), half)
    for slot, block in enumerate((lax.axis_index("y"), 0, 1)):
        o_ref[slot] = own_ref[block, rows, :]


def rows_kernel(own_ref, mine_ref, other_ref, o_ref):
    y = lax.axis_index("y")
    first = lax.axis_index("k") == 0
    n = own_ref.shape[1]

    def block(slot):
        a, b = mine_ref[slot], other_ref[slot]
        return jnp.concatenate([jnp.where(first, a, b), jnp.where(first, b, a)], axis=0)

    diag = own_ref[y]
    a = mul(own_ref[:3].reshape(3 * n, n), diag)
    zero = jnp.zeros_like(diag)
    near, far = block(0), block(3)
    y2 = jnp.where(y > 2, -mul(near, a[2 * n :]), zero)
    t1 = a[n : 2 * n] + mul(block(2), y2)
    y1 = jnp.where(y > 1, -mul(jnp.where(y > 2, far, near), t1), zero)
    t0 = a[:n] + mul(jnp.where(y > 2, block(4), block(1)), y1) + mul(block(1), y2)
    y0 = jnp.where(y > 0, -mul(jnp.where(y > 2, block(5), jnp.where(y > 1, far, near)), t0), zero)
    for m, value in enumerate((y0, y1, y2, zero)):
        o_ref[m] = jnp.where(y == m, diag, value)


def solve_kernel(j, right_ref, inv_ref, *refs):
    new_ref, sent_ref = refs[-2:]
    value = jnp.zeros(new_ref.shape, jnp.float32)
    for m in range(4):
        right = right_ref[m] if j == 0 else sum(right_ref[s, m] for s in range(4))
        value = value + mul(right, inv_ref[m])
    if j > 0:
        value = jnp.where(lax.axis_index("x") == j, value, refs[0][...])
    new_ref[...] = value
    for to in range(4):
        sent_ref[to] = value


def gram_kernel(all_ref, own_ref, o_ref):
    every = all_ref[...].reshape(-1, own_ref.shape[1])
    o_ref[...] = lax.dot_general(own_ref[...], every, (((1,), (1,)), ((), ())), precision=HI, preferred_element_type=jnp.float32)


def split_kernel(near_ref, all_ref, own_ref, o_ref):
    qc = own_ref.shape[0]
    every = all_ref[...].reshape(-1, own_ref.shape[1])
    far = lax.dot_general(own_ref[...], every, (((1,), (1,)), ((), ())), precision=HI, preferred_element_type=jnp.float32)
    near = near_ref[...]
    lane = lax.broadcasted_iota(jnp.int32, (qc, 128), 1)
    for c in range(16):
        at = c * qc // 128 * 128
        shift = c * qc % 128
        a = pltpu.roll(near[:, at : at + 128], (128 - shift) % 128, 1)
        b = pltpu.roll(far[:, at : at + 128], (128 - shift + qc) % 128, 1)
        o_ref[c] = jnp.where(lane < qc, a, b)


def final_kernel(part_ref, prior_ref, query_ref, o_ref):
    total = part_ref[0]
    for s in range(1, part_ref.shape[0]):
        total = total + part_ref[s]
    qc = total.shape[0]
    lane = lax.broadcasted_iota(jnp.int32, total.shape, 1)
    turned = jnp.where(lane < qc, pltpu.roll(total, 128 - qc, 1), pltpu.roll(total, qc, 1))
    total = jnp.where(lax.axis_index("k") == 0, total, turned)
    o_ref[...] = query_ref[...] - (prior_ref[...] + total[:, : 2 * qc])


def update_kernel(j, got_ref, panel_ref, old_ref, new_ref, sent_ref):
    known = got_ref[j]
    for m in range(4):
        old = jnp.where(lax.axis_index("y") == m, old_ref[...], 0.0) if j == 0 else old_ref[m]
        value = old - mul(known, panel_ref[0, m])
        new_ref[m] = value
        for to in range(4):
            sent_ref[to, m] = value


def update(j, got, panels, old):
    qc, n = got.shape[1:]
    whole = lambda a: pl.BlockSpec(a.shape, lambda i: (0,) * a.ndim)
    outs = (f32(4, qc, n), f32(4, 4, qc, n))
    return pl.pallas_call(
        functools.partial(update_kernel, j),
        out_shape=outs,
        grid=(1,),
        in_specs=[whole(got), pl.BlockSpec((1,) + panels.shape[1:], lambda i: (j, 0, 0, 0)), whole(old)],
        out_specs=tuple(whole(o) for o in outs),
        cost_estimate=pl.CostEstimate(flops=12 * 4 * qc * n * n, bytes_accessed=4 * 4 * n * n + 24 * 4 * qc * n, transcendentals=0),
        compiler_params=pltpu.CompilerParams(vmem_limit_bytes=GRANT),
        name=f"update{j}",
    )(got, panels, old)


def body(l_rows, v_prev, l_tail, k_cross, k_query):
    x_id, y_id, k_id = lax.axis_index("x"), lax.axis_index("y"), lax.axis_index("k")
    zh_id, zl_id = lax.axis_index("zh"), lax.axis_index("zl")
    rows = l_rows.shape[0]
    qc = k_cross.shape[1]

    with jax.named_scope("gather_l"):
        block = l_tail.T
        turn = [
            (((x * 4 + y) * 4 + h) * 4 + l, ((x * 4 + l) * 4 + h) * 4 + y)
            for x in range(4) for y in range(4) for h in range(4) for l in range(4) if h != x
        ]
        other = swap(block)
        turned = lax.ppermute(block, ("x", "y", "zh", "zl"), turn)
        inverted = invert(block, other)
        block = jnp.where(zh_id == x_id, jnp.where(zl_id == y_id, inverted, block), turned)
        panels = lax.all_gather(block, ("zh", "zl", "k"), axis=0)
        panels = panels.reshape(4, 4, rows, rows)

    with jax.named_scope("stage1"):
        vt = v_prev.T
        vt_other = swap(vt)
        l_other = swap(l_rows)
        v_pair = jnp.concatenate([vt, vt_other], axis=1)
        l_pair = jnp.concatenate([l_rows, l_other], axis=1)
        v_half = lax.dynamic_slice_in_dim(v_pair, k_id * qc, qc, 0)
        v_all = share(v_half, PLANE_T, 16)
        update_all = contract(v_all, l_pair, ((2,), (1,)))
        prior = contract(v_all, v_pair, ((2,), (1,)))

        panels, prior = lax.optimization_barrier((panels, prior))
        prior = lax.psum_scatter(prior.reshape(16 * qc, -1), ("zl", "zh"), scatter_dimension=0, tiled=True)

    with jax.named_scope("reduce_z"):
        both = lax.all_to_all(update_all.reshape(4, 4, qc, rows), "zl", 0, 0).sum(0)
        both = lax.all_to_all(both, "zh", 0, 0).sum(0)
        rest = k_cross.T - both

    with jax.named_scope("inverse"):
        own = lax.dynamic_slice_in_dim(panels, x_id, 1, 0)[0]
        sent = local(pack_kernel, f32(3, rows // 2, rows), "pack", own)
        got = [
            lax.ppermute(sent[: 3 - d], "y", [(y, y + 1 + d) for y in range(3 - d)]) for d in range(3)
        ]
        mine = jnp.concatenate(got, axis=0)
        theirs = swap(mine)
        inverse = local(rows_kernel, f32(4, rows, rows), "inverse_rows", own, mine, theirs, flops=8 * 12 * rows**3)

    partial_rest = rest
    right = share(rest, "y", 4)
    solved = ()
    for j in range(4):
        with jax.named_scope(f"solve{j}"):
            if j == 3:
                right, prior = lax.optimization_barrier((right, prior))
            solved, sent = local(
                functools.partial(solve_kernel, j), (f32(qc, rows), f32(4, qc, rows)), f"solve{j}",
                right, inverse, *solved, flops=12 * 4 * qc * rows * rows,
            )
            if j < 3:
                solved = (solved,)
                got = lax.all_to_all(sent, "x", 0, 0)
                partial_rest, sent = update(j, got, panels, partial_rest)
                right = lax.all_to_all(sent, "y", 0, 0)

    with jax.named_scope("gram"):
        near = lax.all_to_all(sent, "zh", 0, 0)
        near = share(near, "zl", 4)
        far = swap(near)
        flops = 12 * 16 * qc * qc * rows
        part = local(gram_kernel, f32(qc, 16 * qc), "gram_near", near, solved, flops=flops)
        part = local(split_kernel, f32(16, qc, 128), "gram_far", part, far, solved, flops=flops)
        part = lax.all_to_all(part, PLANE_T, 0, 0)
        posterior = local(final_kernel, f32(qc, 2 * qc), "final", part, prior, k_query.T).T
    return solved.T, posterior


def solution(mesh):
    fine = Mesh(mesh.devices.reshape(4, 4, 4, 4, 2), ("x", "y", "zh", "zl", "k"))
    row, col = ("x", "y"), ("zh", "zl", "k")
    in_specs = (P(row, col), P(col, row), P(row, col), P(row, col), P(row, col))
    return jax.shard_map(body, mesh=fine, in_specs=in_specs, out_specs=(P(row, col), P(row, col)), check_vma=False)
```

```python
import functools
import jax
import jax.numpy as jnp
from jax import lax
from jax.experimental import pallas as pl
from jax.experimental.pallas import tpu as pltpu
from jax.sharding import Mesh, PartitionSpec as P


HI = lax.Precision.HIGHEST
PLANE_T = ("y", "x")
GRANT = 16 * 1024 * 1024
VMEM = pl.BlockSpec(memory_space=pltpu.VMEM)


def contract(a, b, dims):
    return lax.dot_general(a, b, (dims, ((), ())), precision=HI, preferred_element_type=jnp.float32)


def mul(a, b):
    return jnp.dot(a, b, precision=HI, preferred_element_type=jnp.float32)


def share(value, axis, count):
    return lax.all_to_all(jnp.broadcast_to(value[None], (count,) + value.shape), axis, 0, 0)


def swap(value):
    return lax.ppermute(value, "k", [(0, 1), (1, 0)])


def f32(*shape):
    return jax.ShapeDtypeStruct(shape, jnp.float32)


def local(kernel, out_shape, *operands, flops=0):
    outs = out_shape if isinstance(out_shape, tuple) else (out_shape,)
    moved = sum(4 * o.size for o in operands) + sum(4 * o.size for o in outs)
    return pl.pallas_call(
        kernel,
        out_shape=out_shape,
        in_specs=[VMEM] * len(operands),
        out_specs=tuple(VMEM for _ in outs) if isinstance(out_shape, tuple) else VMEM,
        cost_estimate=pl.CostEstimate(flops=flops, bytes_accessed=moved, transcendentals=0),
        compiler_params=pltpu.CompilerParams(vmem_limit_bytes=GRANT),
    )(*operands)


def invert_kernel(own_ref, other_ref, o_ref, full):
    first = lax.axis_index("k") == 0
    a, b = own_ref[...], other_ref[...]
    u = jnp.concatenate([jnp.where(first, a, b), jnp.where(first, b, a)], axis=0)
    n = u.shape[0]
    row = lax.broadcasted_iota(jnp.int32, (n, n), 0)
    col = lax.broadcasted_iota(jnp.int32, (n, n), 1)
    x = jnp.where(row == col, 1.0 / u, 0.0)
    s = 0
    while (1 << s) < n:
        above = ((row >> (s + 1)) == (col >> (s + 1))) & (((row >> s) & 1) == 0) & (((col >> s) & 1) == 1)
        x = x - mul(mul(x, jnp.where(above, u, 0.0)), x)
        s += 1
    full[...] = x
    half = o_ref.shape[0]
    o_ref[...] = full[pl.ds(pl.multiple_of(lax.axis_index("k") * half, half), half), :]


def invert(own, other):
    half, n = own.shape
    return pl.pallas_call(
        invert_kernel,
        out_shape=f32(half, n),
        in_specs=[VMEM, VMEM],
        out_specs=VMEM,
        scratch_shapes=[pltpu.VMEM((n, n), jnp.float32)],
        cost_estimate=pl.CostEstimate(flops=32 * 6 * n * n * n, bytes_accessed=12 * half * n, transcendentals=0),
        compiler_params=pltpu.CompilerParams(vmem_limit_bytes=GRANT),
        name="invert_block",
    )(own, other)


def pack_kernel(own_ref, o_ref):
    half = o_ref.shape[1]
    rows = pl.ds(pl.multiple_of(lax.axis_index("k") * half, half), half)
    for slot, block in enumerate((lax.axis_index("y"), 0, 1)):
        o_ref[slot] = own_ref[block, rows, :]


def rows_kernel(own_ref, mine_ref, other_ref, o_ref):
    y = lax.axis_index("y")
    first = lax.axis_index("k") == 0
    n = own_ref.shape[1]

    def block(slot):
        a, b = mine_ref[slot], other_ref[slot]
        return jnp.concatenate([jnp.where(first, a, b), jnp.where(first, b, a)], axis=0)

    diag = own_ref[y]
    a = mul(own_ref[:3].reshape(3 * n, n), diag)
    zero = jnp.zeros_like(diag)
    near, far = block(0), block(3)
    y2 = jnp.where(y > 2, -mul(near, a[2 * n :]), zero)
    t1 = a[n : 2 * n] + mul(block(2), y2)
    y1 = jnp.where(y > 1, -mul(jnp.where(y > 2, far, near), t1), zero)
    t0 = a[:n] + mul(jnp.where(y > 2, block(4), block(1)), y1) + mul(block(1), y2)
    y0 = jnp.where(y > 0, -mul(jnp.where(y > 2, block(5), jnp.where(y > 1, far, near)), t0), zero)
    for m, value in enumerate((y0, y1, y2, zero)):
        o_ref[m] = jnp.where(y == m, diag, value)


def solve_kernel(j, right_ref, inv_ref, *refs):
    new_ref, sent_ref = refs[-2:]
    value = jnp.zeros(new_ref.shape, jnp.float32)
    for m in range(4):
        right = right_ref[m] if j == 0 else sum(right_ref[s, m] for s in range(4))
        value = value + mul(right, inv_ref[m])
    if j > 0:
        value = jnp.where(lax.axis_index("x") == j, value, refs[0][...])
    new_ref[...] = value
    for to in range(4):
        sent_ref[to] = value


def gram_kernel(all_ref, own_ref, o_ref):
    every = all_ref[...].reshape(-1, own_ref.shape[1])
    o_ref[...] = lax.dot_general(own_ref[...], every, (((1,), (1,)), ((), ())), precision=HI, preferred_element_type=jnp.float32)


def split_kernel(near_ref, all_ref, own_ref, o_ref):
    qc = own_ref.shape[0]
    every = all_ref[...].reshape(-1, own_ref.shape[1])
    far = lax.dot_general(own_ref[...], every, (((1,), (1,)), ((), ())), precision=HI, preferred_element_type=jnp.float32)
    near = near_ref[...]
    lane = lax.broadcasted_iota(jnp.int32, (qc, 128), 1)
    for c in range(16):
        at = c * qc // 128 * 128
        shift = c * qc % 128
        a = pltpu.roll(near[:, at : at + 128], (128 - shift) % 128, 1)
        b = pltpu.roll(far[:, at : at + 128], (128 - shift + qc) % 128, 1)
        value = jnp.where(lane < qc, a, b)
        low = pltpu.roll(value[qc // 2 :], 64, 1)
        o_ref[c] = jnp.where(lane[: qc // 2] < 2 * qc, value[: qc // 2], low)


def final_kernel(part_ref, prior_ref, query_ref, o_ref):
    total = part_ref[0]
    for s in range(1, part_ref.shape[0]):
        total = total + part_ref[s]
    total = jnp.concatenate([total, pltpu.roll(total, 64, 1)], axis=0)
    qc = total.shape[0]
    lane = lax.broadcasted_iota(jnp.int32, total.shape, 1)
    turned = jnp.where(lane < qc, pltpu.roll(total, 128 - qc, 1), pltpu.roll(total, qc, 1))
    total = jnp.where(lax.axis_index("k") == 0, total, turned)
    o_ref[...] = query_ref[...] - (prior_ref[...] + total[:, : 2 * qc])


def update_kernel(j, got_ref, panel_ref, old_ref, new_ref, sent_ref, held, sems):
    copies = [pltpu.make_async_copy(panel_ref.at[j, m], held.at[m], sems.at[m]) for m in range(4)]
    for copy in copies:
        copy.start()
    known = got_ref[j]
    for m in range(4):
        old = jnp.where(lax.axis_index("y") == m, old_ref[...], 0.0) if j == 0 else old_ref[m]
        copies[m].wait()
        value = old - mul(known, held[m])
        new_ref[m] = value
        for to in range(4):
            sent_ref[to, m] = value


def update(j, got, panels, old):
    qc, n = got.shape[1:]
    return pl.pallas_call(
        functools.partial(update_kernel, j),
        out_shape=(f32(4, qc, n), f32(4, 4, qc, n)),
        in_specs=[VMEM, pl.BlockSpec(memory_space=pltpu.HBM), VMEM],
        out_specs=(VMEM, VMEM),
        scratch_shapes=[pltpu.VMEM((4, n, n), jnp.float32), pltpu.SemaphoreType.DMA((4,))],
        cost_estimate=pl.CostEstimate(flops=12 * 4 * qc * n * n, bytes_accessed=4 * 4 * n * n + 24 * 4 * qc * n, transcendentals=0),
        compiler_params=pltpu.CompilerParams(vmem_limit_bytes=GRANT),
    )(got, pltpu.with_memory_space_constraint(panels, pltpu.HBM), old)


def body(l_rows, v_prev, l_tail, k_cross, k_query):
    x_id, y_id, k_id = lax.axis_index("x"), lax.axis_index("y"), lax.axis_index("k")
    zh_id, zl_id = lax.axis_index("zh"), lax.axis_index("zl")
    rows = l_rows.shape[0]
    qc = k_cross.shape[1]

    block = l_tail.T
    turn = [
        (((x * 4 + y) * 4 + h) * 4 + l, ((x * 4 + l) * 4 + h) * 4 + y)
        for x in range(4) for y in range(4) for h in range(4) for l in range(4) if h != x
    ]
    other = swap(block)
    turned = lax.ppermute(block, ("x", "y", "zh", "zl"), turn)
    inverted = invert(block, other)
    block = jnp.where(zh_id == x_id, jnp.where(zl_id == y_id, inverted, block), turned)
    panels = lax.all_gather(block, ("zh", "zl", "k"), axis=0)
    panels = panels.reshape(4, 4, rows, rows)

    vt = v_prev.T
    vt_other = swap(vt)
    l_other = swap(l_rows)
    v_pair = jnp.concatenate([vt, vt_other], axis=1)
    l_pair = jnp.concatenate([l_rows, l_other], axis=1)
    v_half = lax.dynamic_slice_in_dim(v_pair, k_id * qc, qc, 0)
    v_all = share(v_half, PLANE_T, 16)
    update_all = contract(v_all, l_pair, ((2,), (1,)))
    prior = contract(v_all, v_pair, ((2,), (1,)))


    both = jnp.concatenate([update_all, prior], axis=2).reshape(4, 4, qc, -1)
    both = lax.all_to_all(both, "zl", 0, 0).sum(0)
    panels, both = lax.optimization_barrier((panels, both))
    both = lax.all_to_all(both, "zh", 0, 0)
    both = both.sum(0)
    rest = k_cross.T - both[:, :rows]
    prior = both[:, rows:]

    own = lax.dynamic_slice_in_dim(panels, x_id, 1, 0)[0]
    sent = local(pack_kernel, f32(3, rows // 2, rows), own)
    got = [
        lax.ppermute(sent[: 3 - d], "y", [(y, y + 1 + d) for y in range(3 - d)]) for d in range(3)
    ]
    mine = jnp.concatenate(got, axis=0)
    theirs = swap(mine)
    inverse = local(rows_kernel, f32(4, rows, rows), own, mine, theirs, flops=8 * 12 * rows**3)

    partial_rest = rest
    right = share(rest, "y", 4)
    solved = ()
    for j in range(4):
        solved, sent = local(
            functools.partial(solve_kernel, j), (f32(qc, rows), f32(4, qc, rows)),
            right, inverse, *solved, flops=12 * 4 * qc * rows * rows,
        )
        if j < 3:
            solved = (solved,)
            got = lax.all_to_all(sent, "x", 0, 0)
            partial_rest, sent = update(j, got, panels, partial_rest)
            right = lax.all_to_all(sent, "y", 0, 0)

    near = lax.all_to_all(sent, "zh", 0, 0)
    near = share(near, "zl", 4)
    far = swap(near)
    flops = 12 * 16 * qc * qc * rows
    part = local(gram_kernel, f32(qc, 16 * qc), near, solved, flops=flops)
    part = local(split_kernel, f32(16, qc // 2, 128), part, far, solved, flops=flops)
    part = lax.all_to_all(part, PLANE_T, 0, 0)
    posterior = local(final_kernel, f32(qc, 2 * qc), part, prior, k_query.T).T
    return solved.T, posterior


def solution(mesh):
    fine = Mesh(mesh.devices.reshape(4, 4, 4, 4, 2), ("x", "y", "zh", "zl", "k"))
    row, col = ("x", "y"), ("zh", "zl", "k")
    in_specs = (P(row, col), P(col, row), P(row, col), P(row, col), P(row, col))
    return jax.shard_map(body, mesh=fine, in_specs=in_specs, out_specs=(P(row, col), P(row, col)), check_vma=False)
```

```python
import functools
import jax
import jax.numpy as jnp
from jax import lax
from jax.experimental import pallas as pl
from jax.experimental.pallas import tpu as pltpu
from jax.sharding import Mesh, PartitionSpec as P


HI = lax.Precision.HIGHEST
PLANE_T = ("y", "x")
GRANT = 16 * 1024 * 1024
VMEM = pl.BlockSpec(memory_space=pltpu.VMEM)


def contract(a, b, dims):
    return lax.dot_general(a, b, (dims, ((), ())), precision=HI, preferred_element_type=jnp.float32)


def mul(a, b):
    return jnp.dot(a, b, precision=HI, preferred_element_type=jnp.float32)


def share(value, axis, count):
    return lax.all_to_all(jnp.broadcast_to(value[None], (count,) + value.shape), axis, 0, 0)


def swap(value):
    return lax.ppermute(value, "k", [(0, 1), (1, 0)])


def f32(*shape):
    return jax.ShapeDtypeStruct(shape, jnp.float32)


def local(kernel, out_shape, *operands, flops=0):
    outs = out_shape if isinstance(out_shape, tuple) else (out_shape,)
    moved = sum(4 * o.size for o in operands) + sum(4 * o.size for o in outs)
    return pl.pallas_call(
        kernel,
        out_shape=out_shape,
        in_specs=[VMEM] * len(operands),
        out_specs=tuple(VMEM for _ in outs) if isinstance(out_shape, tuple) else VMEM,
        cost_estimate=pl.CostEstimate(flops=flops, bytes_accessed=moved, transcendentals=0),
        compiler_params=pltpu.CompilerParams(vmem_limit_bytes=GRANT),
    )(*operands)


def invert_kernel(own_ref, other_ref, o_ref, full):
    first = lax.axis_index("k") == 0
    a, b = own_ref[...], other_ref[...]
    u = jnp.concatenate([jnp.where(first, a, b), jnp.where(first, b, a)], axis=0)
    n = u.shape[0] // 2
    row = lax.broadcasted_iota(jnp.int32, (n, n), 0)
    col = lax.broadcasted_iota(jnp.int32, (n, n), 1)
    us = [u[:n, :n], u[n:, n:]]
    xs = [jnp.where(row == col, 1.0 / v, 0.0) for v in us]
    s = 0
    while (1 << s) < n:
        above = ((row >> (s + 1)) == (col >> (s + 1))) & (((row >> s) & 1) == 0) & (((col >> s) & 1) == 1)
        ts = [mul(x, jnp.where(above, v, 0.0)) for x, v in zip(xs, us)]
        xs = [x - mul(t, x) for x, t in zip(xs, ts)]
        s += 1
    full[:n, :n] = xs[0]
    full[n:, n:] = xs[1]
    full[:n, n:] = -mul(mul(xs[0], u[:n, n:]), xs[1])
    full[n:, :n] = jnp.zeros((n, n), jnp.float32)
    half = o_ref.shape[0]
    o_ref[...] = full[pl.ds(pl.multiple_of(lax.axis_index("k") * half, half), half), :]


def invert(own, other):
    half, n = own.shape
    return pl.pallas_call(
        invert_kernel,
        out_shape=f32(half, n),
        in_specs=[VMEM, VMEM],
        out_specs=VMEM,
        scratch_shapes=[pltpu.VMEM((n, n), jnp.float32)],
        cost_estimate=pl.CostEstimate(flops=32 * 6 * n * n * n, bytes_accessed=12 * half * n, transcendentals=0),
        compiler_params=pltpu.CompilerParams(vmem_limit_bytes=GRANT),
        name="invert_block",
    )(own, other)


def copy_kernel(a_ref, o_ref):
    o_ref[...] = a_ref[...]


def pack_kernel(own_ref, o_ref):
    half = o_ref.shape[1]
    rows = pl.ds(pl.multiple_of(lax.axis_index("k") * half, half), half)
    for slot, block in enumerate((lax.axis_index("y"), 0, 1)):
        o_ref[slot] = own_ref[block, rows, :]


def rows_kernel(own_ref, mine_ref, other_ref, o_ref):
    y = lax.axis_index("y")
    first = lax.axis_index("k") == 0
    n = own_ref.shape[1]

    def block(slot):
        a, b = mine_ref[slot], other_ref[slot]
        return jnp.concatenate([jnp.where(first, a, b), jnp.where(first, b, a)], axis=0)

    diag = own_ref[y]
    a = mul(own_ref[:3].reshape(3 * n, n), diag)
    zero = jnp.zeros_like(diag)
    near, far = block(0), block(3)
    y2 = jnp.where(y > 2, -mul(near, a[2 * n :]), zero)
    t1 = a[n : 2 * n] + mul(block(2), y2)
    y1 = jnp.where(y > 1, -mul(jnp.where(y > 2, far, near), t1), zero)
    t0 = a[:n] + mul(jnp.where(y > 2, block(4), block(1)), y1) + mul(block(1), y2)
    y0 = jnp.where(y > 0, -mul(jnp.where(y > 2, block(5), jnp.where(y > 1, far, near)), t0), zero)
    for m, value in enumerate((y0, y1, y2, zero)):
        o_ref[m] = jnp.where(y == m, diag, value)


def solve_kernel(j, right_ref, inv_ref, *refs):
    new_ref, sent_ref = refs[-2:]
    value = jnp.zeros(new_ref.shape, jnp.float32)
    for m in range(4):
        right = right_ref[m] if j == 0 else sum(right_ref[s, m] for s in range(4))
        value = value + mul(right, inv_ref[m])
    if j > 0:
        value = jnp.where(lax.axis_index("x") == j, value, refs[0][...])
    new_ref[...] = value
    for to in range(4):
        sent_ref[to] = value


def gram_kernel(all_ref, own_ref, o_ref):
    every = all_ref[...].reshape(-1, own_ref.shape[1])
    o_ref[...] = lax.dot_general(own_ref[...], every, (((1,), (1,)), ((), ())), precision=HI, preferred_element_type=jnp.float32)


def split_kernel(near_ref, all_ref, own_ref, o_ref):
    qc = own_ref.shape[0]
    every = all_ref[...].reshape(-1, own_ref.shape[1])
    far = lax.dot_general(own_ref[...], every, (((1,), (1,)), ((), ())), precision=HI, preferred_element_type=jnp.float32)
    near = near_ref[...]
    lane = lax.broadcasted_iota(jnp.int32, (qc, 128), 1)
    for c in range(16):
        at = c * qc // 128 * 128
        shift = c * qc % 128
        a = pltpu.roll(near[:, at : at + 128], (128 - shift) % 128, 1)
        b = pltpu.roll(far[:, at : at + 128], (128 - shift + qc) % 128, 1)
        value = jnp.where(lane < qc, a, b)
        low = pltpu.roll(value[qc // 2 :], 64, 1)
        o_ref[c] = jnp.where(lane[: qc // 2] < 2 * qc, value[: qc // 2], low)


def final_kernel(part_ref, prior_ref, query_ref, o_ref):
    total = part_ref[0]
    for s in range(1, part_ref.shape[0]):
        total = total + part_ref[s]
    total = jnp.concatenate([total, pltpu.roll(total, 64, 1)], axis=0)
    qc = total.shape[0]
    lane = lax.broadcasted_iota(jnp.int32, total.shape, 1)
    turned = jnp.where(lane < qc, pltpu.roll(total, 128 - qc, 1), pltpu.roll(total, qc, 1))
    total = jnp.where(lax.axis_index("k") == 0, total, turned)
    o_ref[...] = query_ref[...] - (prior_ref[...] + total[:, : 2 * qc])


def update_kernel(j, got_ref, panel_ref, old_ref, new_ref, sent_ref):
    known = got_ref[j]
    for m in range(4):
        old = jnp.where(lax.axis_index("y") == m, old_ref[...], 0.0) if j == 0 else old_ref[m]
        value = old - mul(known, panel_ref[0, m])
        new_ref[m] = value
        for to in range(4):
            sent_ref[to, m] = value


def update(j, got, panels, old):
    qc, n = got.shape[1:]
    whole = lambda a: pl.BlockSpec(a.shape, lambda i: (0,) * a.ndim)
    outs = (f32(4, qc, n), f32(4, 4, qc, n))
    return pl.pallas_call(
        functools.partial(update_kernel, j),
        out_shape=outs,
        grid=(1,),
        in_specs=[whole(got), pl.BlockSpec((1,) + panels.shape[1:], lambda i: (j, 0, 0, 0)), whole(old)],
        out_specs=tuple(whole(o) for o in outs),
        cost_estimate=pl.CostEstimate(flops=12 * 4 * qc * n * n, bytes_accessed=4 * 4 * n * n + 24 * 4 * qc * n, transcendentals=0),
        compiler_params=pltpu.CompilerParams(vmem_limit_bytes=GRANT),
    )(got, pltpu.with_memory_space_constraint(panels, pltpu.HBM), old)


def body(l_rows, v_prev, l_tail, k_cross, k_query):
    x_id, y_id, k_id = lax.axis_index("x"), lax.axis_index("y"), lax.axis_index("k")
    zh_id, zl_id = lax.axis_index("zh"), lax.axis_index("zl")
    rows = l_rows.shape[0]
    qc = k_cross.shape[1]

    block = l_tail.T
    turn = [
        (((x * 4 + y) * 4 + h) * 4 + l, ((x * 4 + l) * 4 + h) * 4 + y)
        for x in range(4) for y in range(4) for h in range(4) for l in range(4) if h != x
    ]
    other = swap(block)
    turned = lax.ppermute(block, ("x", "y", "zh", "zl"), turn)
    inverted = invert(block, other)
    block = jnp.where(zh_id == x_id, jnp.where(zl_id == y_id, inverted, block), turned)
    panels = lax.all_gather(block, ("zh", "zl", "k"), axis=0)
    panels = panels.reshape(4, 4, rows, rows)

    vt = v_prev.T
    vt_other = swap(vt)
    l_other = swap(l_rows)
    v_pair = jnp.concatenate([vt, vt_other], axis=1)
    l_pair = jnp.concatenate([l_rows, l_other], axis=1)
    v_half = lax.dynamic_slice_in_dim(v_pair, k_id * qc, qc, 0)
    v_all = share(v_half, PLANE_T, 16)
    update_all = contract(v_all, l_pair, ((2,), (1,)))
    prior = contract(v_all, v_pair, ((2,), (1,)))


    both = jnp.concatenate([update_all, prior], axis=2).reshape(4, 4, qc, -1)
    both = lax.all_to_all(both, "zl", 0, 0).sum(0)
    both = lax.all_to_all(both, "zh", 0, 0)
    both = both.sum(0)
    cross = local(copy_kernel, f32(qc, rows), k_cross.T)
    rest = cross - both[:, :rows]
    prior = both[:, rows:]

    own = lax.dynamic_slice_in_dim(panels, x_id, 1, 0)[0]
    sent = local(pack_kernel, f32(3, rows // 2, rows), own)
    got = [
        lax.ppermute(sent[: 3 - d], "y", [(y, y + 1 + d) for y in range(3 - d)]) for d in range(3)
    ]
    mine = jnp.concatenate(got, axis=0)
    theirs = swap(mine)
    inverse = local(rows_kernel, f32(4, rows, rows), own, mine, theirs, flops=8 * 12 * rows**3)

    partial_rest = rest
    right = share(rest, "y", 4)
    solved = ()
    for j in range(4):
        solved, sent = local(
            functools.partial(solve_kernel, j), (f32(qc, rows), f32(4, qc, rows)),
            right, inverse, *solved, flops=12 * 4 * qc * rows * rows,
        )
        if j < 3:
            solved = (solved,)
            got = lax.all_to_all(sent, "x", 0, 0)
            partial_rest, sent = update(j, got, panels, partial_rest)
            right = lax.all_to_all(sent, "y", 0, 0)

    near = lax.all_to_all(sent, "zh", 0, 0)
    near = share(near, "zl", 4)
    far = swap(near)
    flops = 12 * 16 * qc * qc * rows
    part = local(gram_kernel, f32(qc, 16 * qc), near, solved, flops=flops)
    part = local(split_kernel, f32(16, qc // 2, 128), part, far, solved, flops=flops)
    part = lax.all_to_all(part, PLANE_T, 0, 0)
    posterior = local(final_kernel, f32(qc, 2 * qc), part, prior, k_query.T).T
    return solved.T, posterior


def solution(mesh):
    fine = Mesh(mesh.devices.reshape(4, 4, 4, 4, 2), ("x", "y", "zh", "zl", "k"))
    row, col = ("x", "y"), ("zh", "zl", "k")
    in_specs = (P(row, col), P(col, row), P(row, col), P(row, col), P(row, col))
    return jax.shard_map(body, mesh=fine, in_specs=in_specs, out_specs=(P(row, col), P(row, col)), check_vma=False)
```

```python
import functools
import jax
import jax.numpy as jnp
from jax import lax
from jax.experimental import pallas as pl
from jax.experimental.pallas import tpu as pltpu
from jax.sharding import Mesh, PartitionSpec as P


HI = lax.Precision.HIGHEST
PLANE_T = ("y", "x")
GRANT = 16 * 1024 * 1024
VMEM = pl.BlockSpec(memory_space=pltpu.VMEM)


def contract(a, b, dims):
    return lax.dot_general(a, b, (dims, ((), ())), precision=HI, preferred_element_type=jnp.float32)


def mul(a, b):
    return jnp.dot(a, b, precision=HI, preferred_element_type=jnp.float32)


def share(value, axis, count):
    return lax.all_to_all(jnp.broadcast_to(value[None], (count,) + value.shape), axis, 0, 0)


def swap(value):
    return lax.ppermute(value, "k", [(0, 1), (1, 0)])


def f32(*shape):
    return jax.ShapeDtypeStruct(shape, jnp.float32)


def local(kernel, out_shape, *operands, flops=0):
    outs = out_shape if isinstance(out_shape, tuple) else (out_shape,)
    moved = sum(4 * o.size for o in operands) + sum(4 * o.size for o in outs)
    return pl.pallas_call(
        kernel,
        out_shape=out_shape,
        in_specs=[VMEM] * len(operands),
        out_specs=tuple(VMEM for _ in outs) if isinstance(out_shape, tuple) else VMEM,
        cost_estimate=pl.CostEstimate(flops=flops, bytes_accessed=moved, transcendentals=0),
        compiler_params=pltpu.CompilerParams(vmem_limit_bytes=GRANT),
    )(*operands)


def invert_kernel(own_ref, other_ref, o_ref, full):
    first = lax.axis_index("k") == 0
    u = joined(first, own_ref[...], other_ref[...])
    n = u.shape[0] // 2
    row = lax.broadcasted_iota(jnp.int32, (n, n), 0)
    col = lax.broadcasted_iota(jnp.int32, (n, n), 1)
    us = [u[:n, :n], u[n:, n:]]
    xs = [jnp.where(row == col, 1.0 / v, 0.0) for v in us]
    s = 0
    while (1 << s) < n:
        above = ((row >> (s + 1)) == (col >> (s + 1))) & (((row >> s) & 1) == 0) & (((col >> s) & 1) == 1)
        ts = [mul(x, jnp.where(above, v, 0.0)) for x, v in zip(xs, us)]
        xs = [x - mul(t, x) for x, t in zip(xs, ts)]
        s += 1
    full[:n, :n] = xs[0]
    full[n:, n:] = xs[1]
    full[:n, n:] = -mul(mul(xs[0], u[:n, n:]), xs[1])
    full[n:, :n] = jnp.zeros((n, n), jnp.float32)
    half = o_ref.shape[0]
    o_ref[...] = full[pl.ds(pl.multiple_of(lax.axis_index("k") * half, half), half), :]


def invert(own, other):
    half, n = own.shape
    return pl.pallas_call(
        invert_kernel,
        out_shape=f32(half, n),
        in_specs=[VMEM, VMEM],
        out_specs=VMEM,
        scratch_shapes=[pltpu.VMEM((n, n), jnp.float32)],
        cost_estimate=pl.CostEstimate(flops=32 * 6 * n * n * n, bytes_accessed=12 * half * n, transcendentals=0),
        compiler_params=pltpu.CompilerParams(vmem_limit_bytes=GRANT),
        name="invert_block",
    )(own, other)


def copy_kernel(a_ref, o_ref):
    o_ref[...] = a_ref[...]


def joined(first, mine, other):
    return jnp.concatenate([jnp.where(first, mine, other), jnp.where(first, other, mine)], axis=0)


def pack_kernel(own_ref, o_ref):
    for slot, block in enumerate((lax.axis_index("y"), 0, 1)):
        o_ref[slot] = own_ref[block]


def rows_kernel(own_ref, own_other_ref, mine_ref, other_ref, o_ref):
    y = lax.axis_index("y")
    first = lax.axis_index("k") == 0
    n = own_ref.shape[2]

    def block(slot):
        return joined(first, mine_ref[slot], other_ref[slot])

    diag = joined(first, own_ref[y], own_other_ref[y])
    a = mul(jnp.concatenate([joined(first, own_ref[m], own_other_ref[m]) for m in range(3)], axis=0), diag)
    zero = jnp.zeros_like(diag)
    near, far = block(0), block(3)
    y2 = jnp.where(y > 2, -mul(near, a[2 * n :]), zero)
    t1 = a[n : 2 * n] + mul(block(2), y2)
    y1 = jnp.where(y > 1, -mul(jnp.where(y > 2, far, near), t1), zero)
    t0 = a[:n] + mul(jnp.where(y > 2, block(4), block(1)), y1) + mul(block(1), y2)
    y0 = jnp.where(y > 0, -mul(jnp.where(y > 2, block(5), jnp.where(y > 1, far, near)), t0), zero)
    for m, value in enumerate((y0, y1, y2, zero)):
        o_ref[m] = jnp.where(y == m, diag, value)


def solve_kernel(j, right_ref, inv_ref, *refs):
    new_ref, sent_ref = refs[-2:]
    value = jnp.zeros(new_ref.shape, jnp.float32)
    for m in range(4):
        right = right_ref[m] if j == 0 else sum(right_ref[s, m] for s in range(4))
        value = value + mul(right, inv_ref[m])
    if j > 0:
        value = jnp.where(lax.axis_index("x") == j, value, refs[0][...])
    new_ref[...] = value
    for to in range(4):
        sent_ref[to] = value


def gram_kernel(all_ref, own_ref, o_ref):
    every = all_ref[...].reshape(-1, own_ref.shape[1])
    o_ref[...] = lax.dot_general(own_ref[...], every, (((1,), (1,)), ((), ())), precision=HI, preferred_element_type=jnp.float32)


def split_kernel(near_ref, all_ref, own_ref, o_ref):
    qc = own_ref.shape[0]
    every = all_ref[...].reshape(-1, own_ref.shape[1])
    far = lax.dot_general(own_ref[...], every, (((1,), (1,)), ((), ())), precision=HI, preferred_element_type=jnp.float32)
    near = near_ref[...]
    lane = lax.broadcasted_iota(jnp.int32, (qc, 128), 1)
    for c in range(16):
        at = c * qc // 128 * 128
        shift = c * qc % 128
        a = pltpu.roll(near[:, at : at + 128], (128 - shift) % 128, 1)
        b = pltpu.roll(far[:, at : at + 128], (128 - shift + qc) % 128, 1)
        value = jnp.where(lane < qc, a, b)
        low = pltpu.roll(value[qc // 2 :], 64, 1)
        o_ref[c] = jnp.where(lane[: qc // 2] < 2 * qc, value[: qc // 2], low)


def final_kernel(part_ref, prior_ref, query_ref, o_ref):
    total = part_ref[0]
    for s in range(1, part_ref.shape[0]):
        total = total + part_ref[s]
    total = jnp.concatenate([total, pltpu.roll(total, 64, 1)], axis=0)
    qc = total.shape[0]
    lane = lax.broadcasted_iota(jnp.int32, total.shape, 1)
    turned = jnp.where(lane < qc, pltpu.roll(total, 128 - qc, 1), pltpu.roll(total, qc, 1))
    total = jnp.where(lax.axis_index("k") == 0, total, turned)
    o_ref[...] = query_ref[...] - (prior_ref[...] + total[:, : 2 * qc])


def update_kernel(j, got_ref, panel_ref, other_ref, old_ref, new_ref, sent_ref):
    first = lax.axis_index("k") == 0
    known = got_ref[j]
    for m in range(4):
        old = jnp.where(lax.axis_index("y") == m, old_ref[...], 0.0) if j == 0 else old_ref[m]
        value = old - mul(known, joined(first, panel_ref[0, m], other_ref[0, m]))
        new_ref[m] = value
        for to in range(4):
            sent_ref[to, m] = value


def update(j, got, panels, others, old):
    qc, n = got.shape[1:]
    whole = lambda a: pl.BlockSpec(a.shape, lambda i: (0,) * a.ndim)
    outs = (f32(4, qc, n), f32(4, 4, qc, n))
    panel = pl.BlockSpec((1,) + panels.shape[1:], lambda i: (j, 0, 0, 0))
    in_hbm = lambda a: pltpu.with_memory_space_constraint(a, pltpu.HBM)
    return pl.pallas_call(
        functools.partial(update_kernel, j),
        out_shape=outs,
        grid=(1,),
        in_specs=[whole(got), panel, panel, whole(old)],
        out_specs=tuple(whole(o) for o in outs),
        cost_estimate=pl.CostEstimate(flops=12 * 4 * qc * n * n, bytes_accessed=4 * 4 * n * n + 24 * 4 * qc * n, transcendentals=0),
        compiler_params=pltpu.CompilerParams(vmem_limit_bytes=GRANT),
    )(got, in_hbm(panels), in_hbm(others), old)


def body(l_rows, v_prev, l_tail, k_cross, k_query):
    x_id, y_id, k_id = lax.axis_index("x"), lax.axis_index("y"), lax.axis_index("k")
    zh_id, zl_id = lax.axis_index("zh"), lax.axis_index("zl")
    rows = l_rows.shape[0]
    qc = k_cross.shape[1]

    vt = v_prev.T
    vt_other = swap(vt)
    v_pair = jnp.concatenate([vt, vt_other], axis=1)
    v_half = lax.dynamic_slice_in_dim(v_pair, k_id * qc, qc, 0)

    block = l_tail.T
    turn = [
        (((x * 4 + y) * 4 + h) * 4 + l, ((x * 4 + l) * 4 + h) * 4 + y)
        for x in range(4) for y in range(4) for h in range(4) for l in range(4) if h != x
    ]
    other = swap(block)
    turned = lax.ppermute(block, ("x", "y", "zh", "zl"), turn)
    inverted = invert(block, other)
    block = jnp.where(zh_id == x_id, jnp.where(zl_id == y_id, inverted, block), turned)
    block, v_half = lax.optimization_barrier((block, v_half))
    panels = lax.all_gather(block, ("zh", "zl"), axis=0)
    panels = panels.reshape(4, 4, rows // 2, rows)

    l_other = swap(l_rows)
    l_pair = jnp.concatenate([l_rows, l_other], axis=1)
    v_all = share(v_half, PLANE_T, 16)
    update_all = contract(v_all, l_pair, ((2,), (1,)))
    prior = contract(v_all, v_pair, ((2,), (1,)))


    both = jnp.concatenate([update_all, prior], axis=2).reshape(4, 4, qc, -1)
    both = lax.all_to_all(both, "zl", 0, 0).sum(0)
    both = lax.all_to_all(both, "zh", 0, 0)
    both = both.sum(0)
    cross = local(copy_kernel, f32(qc, rows), k_cross.T)
    rest = cross - both[:, :rows]
    prior = both[:, rows:]

    own = lax.dynamic_slice_in_dim(panels, x_id, 1, 0)[0]
    sent = local(pack_kernel, f32(3, rows // 2, rows), own)
    got = [
        lax.ppermute(sent[: 3 - d], "y", [(y, y + 1 + d) for y in range(3 - d)]) for d in range(3)
    ]
    mine = jnp.concatenate(got, axis=0)
    theirs = swap(mine)
    others = swap(panels)
    own_others = lax.dynamic_slice_in_dim(others, x_id, 1, 0)[0]
    inverse = local(rows_kernel, f32(4, rows, rows), own, own_others, mine, theirs, flops=8 * 12 * rows**3)

    partial_rest = rest
    right = share(rest, "y", 4)
    solved = ()
    for j in range(4):
        solved, sent = local(
            functools.partial(solve_kernel, j), (f32(qc, rows), f32(4, qc, rows)),
            right, inverse, *solved, flops=12 * 4 * qc * rows * rows,
        )
        if j < 3:
            solved = (solved,)
            got = lax.all_to_all(sent, "x", 0, 0)
            partial_rest, sent = update(j, got, panels, others, partial_rest)
            right = lax.all_to_all(sent, "y", 0, 0)

    near = lax.all_to_all(sent, "zh", 0, 0)
    near = share(near, "zl", 4)
    far = swap(near)
    flops = 12 * 16 * qc * qc * rows
    part = local(gram_kernel, f32(qc, 16 * qc), near, solved, flops=flops)
    part = local(split_kernel, f32(16, qc // 2, 128), part, far, solved, flops=flops)
    part = lax.all_to_all(part, PLANE_T, 0, 0)
    posterior = local(final_kernel, f32(qc, 2 * qc), part, prior, k_query.T).T
    return solved.T, posterior


def solution(mesh):
    fine = Mesh(mesh.devices.reshape(4, 4, 4, 4, 2), ("x", "y", "zh", "zl", "k"))
    row, col = ("x", "y"), ("zh", "zl", "k")
    in_specs = (P(row, col), P(col, row), P(row, col), P(row, col), P(row, col))
    return jax.shard_map(body, mesh=fine, in_specs=in_specs, out_specs=(P(row, col), P(row, col)), check_vma=False)
```

```python
import functools
import jax
import jax.numpy as jnp
from jax import lax
from jax.experimental import pallas as pl
from jax.experimental.pallas import tpu as pltpu
from jax.sharding import Mesh, PartitionSpec as P


HI = lax.Precision.HIGHEST
PLANE_T = ("y", "x")
GRANT = 16 * 1024 * 1024
VMEM = pl.BlockSpec(memory_space=pltpu.VMEM)


def contract(a, b, dims):
    return lax.dot_general(a, b, (dims, ((), ())), precision=HI, preferred_element_type=jnp.float32)


def mul(a, b):
    return jnp.dot(a, b, precision=HI, preferred_element_type=jnp.float32)


def share(value, axis, count):
    return lax.all_to_all(jnp.broadcast_to(value[None], (count,) + value.shape), axis, 0, 0)


def swap(value):
    return lax.ppermute(value, "k", [(0, 1), (1, 0)])


def f32(*shape):
    return jax.ShapeDtypeStruct(shape, jnp.float32)


def local(kernel, out_shape, *operands, flops=0):
    outs = out_shape if isinstance(out_shape, tuple) else (out_shape,)
    moved = sum(4 * o.size for o in operands) + sum(4 * o.size for o in outs)
    return pl.pallas_call(
        kernel,
        out_shape=out_shape,
        in_specs=[VMEM] * len(operands),
        out_specs=tuple(VMEM for _ in outs) if isinstance(out_shape, tuple) else VMEM,
        cost_estimate=pl.CostEstimate(flops=flops, bytes_accessed=moved, transcendentals=0),
        compiler_params=pltpu.CompilerParams(vmem_limit_bytes=GRANT),
    )(*operands)


def invert_kernel(own_ref, other_ref, o_ref, full):
    first = lax.axis_index("k") == 0
    u = joined(first, own_ref[...], other_ref[...])
    n = u.shape[0] // 2
    row = lax.broadcasted_iota(jnp.int32, (n, n), 0)
    col = lax.broadcasted_iota(jnp.int32, (n, n), 1)
    us = [u[:n, :n], u[n:, n:]]
    xs = [jnp.where(row == col, 1.0 / v, 0.0) for v in us]
    s = 0
    while (1 << s) < n:
        above = ((row >> (s + 1)) == (col >> (s + 1))) & (((row >> s) & 1) == 0) & (((col >> s) & 1) == 1)
        ts = [mul(x, jnp.where(above, v, 0.0)) for x, v in zip(xs, us)]
        xs = [x - mul(t, x) for x, t in zip(xs, ts)]
        s += 1
    full[:n, :n] = xs[0]
    full[n:, n:] = xs[1]
    full[:n, n:] = -mul(mul(xs[0], u[:n, n:]), xs[1])
    full[n:, :n] = jnp.zeros((n, n), jnp.float32)
    half = o_ref.shape[0]
    o_ref[...] = full[pl.ds(pl.multiple_of(lax.axis_index("k") * half, half), half), :]


def invert(own, other):
    half, n = own.shape
    return pl.pallas_call(
        invert_kernel,
        out_shape=f32(half, n),
        in_specs=[VMEM, VMEM],
        out_specs=VMEM,
        scratch_shapes=[pltpu.VMEM((n, n), jnp.float32)],
        cost_estimate=pl.CostEstimate(flops=32 * 6 * n * n * n, bytes_accessed=12 * half * n, transcendentals=0),
        compiler_params=pltpu.CompilerParams(vmem_limit_bytes=GRANT),
        name="invert_block",
    )(own, other)


def copy_kernel(a_ref, o_ref):
    o_ref[...] = a_ref[...]


def joined(first, mine, other):
    return jnp.concatenate([jnp.where(first, mine, other), jnp.where(first, other, mine)], axis=0)


def join_kernel(*refs):
    at = 0
    for ref in refs[:-1]:
        for slot in range(ref.shape[0]):
            refs[-1][at] = ref[slot]
            at += 1


def pack_kernel(own_ref, o_ref):
    for slot, block in enumerate((lax.axis_index("y"), 0, 1)):
        o_ref[slot] = own_ref[block]


def rows_kernel(own_ref, own_other_ref, mine_ref, other_ref, o_ref):
    y = lax.axis_index("y")
    first = lax.axis_index("k") == 0
    n = own_ref.shape[2]

    def block(slot):
        return joined(first, mine_ref[slot], other_ref[slot])

    diag = joined(first, own_ref[y], own_other_ref[y])
    a = mul(jnp.concatenate([joined(first, own_ref[m], own_other_ref[m]) for m in range(3)], axis=0), diag)
    zero = jnp.zeros_like(diag)
    near, far = block(0), block(3)
    y2 = jnp.where(y > 2, -mul(near, a[2 * n :]), zero)
    t1 = a[n : 2 * n] + mul(block(2), y2)
    y1 = jnp.where(y > 1, -mul(jnp.where(y > 2, far, near), t1), zero)
    t0 = a[:n] + mul(jnp.where(y > 2, block(4), block(1)), y1) + mul(block(1), y2)
    y0 = jnp.where(y > 0, -mul(jnp.where(y > 2, block(5), jnp.where(y > 1, far, near)), t0), zero)
    for m, value in enumerate((y0, y1, y2, zero)):
        o_ref[m] = jnp.where(y == m, diag, value)


def solve_kernel(j, right_ref, inv_ref, *refs):
    new_ref, sent_ref = refs[-2:]
    value = jnp.zeros(new_ref.shape, jnp.float32)
    for m in range(4):
        right = right_ref[m] if j == 0 else sum(right_ref[s, m] for s in range(4))
        value = value + mul(right, inv_ref[m])
    if j > 0:
        value = jnp.where(lax.axis_index("x") == j, value, refs[0][...])
    new_ref[...] = value
    for to in range(4):
        sent_ref[to] = value


def gram_kernel(all_ref, own_ref, o_ref):
    every = all_ref[...].reshape(-1, own_ref.shape[1])
    o_ref[...] = lax.dot_general(own_ref[...], every, (((1,), (1,)), ((), ())), precision=HI, preferred_element_type=jnp.float32)


def split_kernel(near_ref, all_ref, own_ref, o_ref):
    qc = own_ref.shape[0]
    every = all_ref[...].reshape(-1, own_ref.shape[1])
    far = lax.dot_general(own_ref[...], every, (((1,), (1,)), ((), ())), precision=HI, preferred_element_type=jnp.float32)
    near = near_ref[...]
    lane = lax.broadcasted_iota(jnp.int32, (qc, 128), 1)
    for c in range(16):
        at = c * qc // 128 * 128
        shift = c * qc % 128
        a = pltpu.roll(near[:, at : at + 128], (128 - shift) % 128, 1)
        b = pltpu.roll(far[:, at : at + 128], (128 - shift + qc) % 128, 1)
        value = jnp.where(lane < qc, a, b)
        low = pltpu.roll(value[qc // 2 :], 64, 1)
        o_ref[c] = jnp.where(lane[: qc // 2] < 2 * qc, value[: qc // 2], low)


def final_kernel(part_ref, prior_ref, query_ref, o_ref):
    total = part_ref[0]
    for s in range(1, part_ref.shape[0]):
        total = total + part_ref[s]
    total = jnp.concatenate([total, pltpu.roll(total, 64, 1)], axis=0)
    qc = total.shape[0]
    lane = lax.broadcasted_iota(jnp.int32, total.shape, 1)
    turned = jnp.where(lane < qc, pltpu.roll(total, 128 - qc, 1), pltpu.roll(total, qc, 1))
    total = jnp.where(lax.axis_index("k") == 0, total, turned)
    o_ref[...] = query_ref[...] - (prior_ref[...] + total[:, : 2 * qc])


def update_kernel(j, got_ref, panel_ref, other_ref, old_ref, new_ref, sent_ref):
    first = lax.axis_index("k") == 0
    known = got_ref[j]
    for m in range(4):
        old = jnp.where(lax.axis_index("y") == m, old_ref[...], 0.0) if j == 0 else old_ref[m]
        value = old - mul(known, joined(first, panel_ref[0, m], other_ref[0, m]))
        new_ref[m] = value
        for to in range(4):
            sent_ref[to, m] = value


def update(j, got, panels, others, old):
    qc, n = got.shape[1:]
    whole = lambda a: pl.BlockSpec(a.shape, lambda i: (0,) * a.ndim)
    outs = (f32(4, qc, n), f32(4, 4, qc, n))
    panel = pl.BlockSpec((1,) + panels.shape[1:], lambda i: (j, 0, 0, 0))
    in_hbm = lambda a: pltpu.with_memory_space_constraint(a, pltpu.HBM)
    return pl.pallas_call(
        functools.partial(update_kernel, j),
        out_shape=outs,
        grid=(1,),
        in_specs=[whole(got), panel, panel, whole(old)],
        out_specs=tuple(whole(o) for o in outs),
        cost_estimate=pl.CostEstimate(flops=12 * 4 * qc * n * n, bytes_accessed=4 * 4 * n * n + 24 * 4 * qc * n, transcendentals=0),
        compiler_params=pltpu.CompilerParams(vmem_limit_bytes=GRANT),
    )(got, in_hbm(panels), in_hbm(others), old)


def body(l_rows, v_prev, l_tail, k_cross, k_query):
    x_id, y_id, k_id = lax.axis_index("x"), lax.axis_index("y"), lax.axis_index("k")
    zh_id, zl_id = lax.axis_index("zh"), lax.axis_index("zl")
    rows = l_rows.shape[0]
    qc = k_cross.shape[1]

    vt = v_prev.T
    vt_other = swap(vt)
    v_pair = jnp.concatenate([vt, vt_other], axis=1)
    v_half = lax.dynamic_slice_in_dim(v_pair, k_id * qc, qc, 0)

    block = l_tail.T
    turn = [
        (((x * 4 + y) * 4 + h) * 4 + l, ((x * 4 + l) * 4 + h) * 4 + y)
        for x in range(4) for y in range(4) for h in range(4) for l in range(4) if h != x
    ]
    other = swap(block)
    turned = lax.ppermute(block, ("x", "y", "zh", "zl"), turn)
    inverted = invert(block, other)
    block = jnp.where(zh_id == x_id, jnp.where(zl_id == y_id, inverted, block), turned)
    block, v_half = lax.optimization_barrier((block, v_half))
    panels = lax.all_gather(block, ("zh", "zl"), axis=0)
    panels = panels.reshape(4, 4, rows // 2, rows)

    l_other = swap(l_rows)
    l_pair = jnp.concatenate([l_rows, l_other], axis=1)
    v_all = share(v_half, PLANE_T, 16)
    update_all = contract(v_all, l_pair, ((2,), (1,)))
    prior = contract(v_all, v_pair, ((2,), (1,)))


    prior = lax.psum_scatter(prior.reshape(16 * qc, -1), ("zl", "zh"), scatter_dimension=0, tiled=True)
    both = lax.all_to_all(update_all.reshape(4, 4, qc, rows), "zl", 0, 0)
    both = both.sum(0)
    both = lax.all_to_all(both, "zh", 0, 0)
    both = both.sum(0)
    cross = local(copy_kernel, f32(qc, rows), k_cross.T)
    rest = cross - both

    own = lax.dynamic_slice_in_dim(panels, x_id, 1, 0)[0]
    sent = local(pack_kernel, f32(3, rows // 2, rows), own)
    got = []
    for d in range(3):
        got.append(lax.ppermute(sent[: 3 - d], "y", [(y, y + 1 + d) for y in range(3 - d)]))
    mine = local(join_kernel, f32(6, rows // 2, rows), *got)
    theirs = swap(mine)
    others = swap(panels)
    own_others = lax.dynamic_slice_in_dim(others, x_id, 1, 0)[0]
    inverse = local(rows_kernel, f32(4, rows, rows), own, own_others, mine, theirs, flops=8 * 12 * rows**3)

    partial_rest = rest
    right = share(rest, "y", 4)
    solved = ()
    for j in range(4):
        solved, sent = local(
            functools.partial(solve_kernel, j), (f32(qc, rows), f32(4, qc, rows)),
            right, inverse, *solved, flops=12 * 4 * qc * rows * rows,
        )
        if j < 3:
            solved = (solved,)
            got = lax.all_to_all(sent, "x", 0, 0)
            partial_rest, sent = update(j, got, panels, others, partial_rest)
            right = lax.all_to_all(sent, "y", 0, 0)

    near = lax.all_to_all(sent, "zh", 0, 0)
    near = share(near, "zl", 4)
    far = swap(near)
    flops = 12 * 16 * qc * qc * rows
    part = local(gram_kernel, f32(qc, 16 * qc), near, solved, flops=flops)
    part = local(split_kernel, f32(16, qc // 2, 128), part, far, solved, flops=flops)
    part = lax.all_to_all(part, PLANE_T, 0, 0)
    posterior = local(final_kernel, f32(qc, 2 * qc), part, prior, k_query.T).T
    return solved.T, posterior


def solution(mesh):
    fine = Mesh(mesh.devices.reshape(4, 4, 4, 4, 2), ("x", "y", "zh", "zl", "k"))
    row, col = ("x", "y"), ("zh", "zl", "k")
    in_specs = (P(row, col), P(col, row), P(row, col), P(row, col), P(row, col))
    return jax.shard_map(body, mesh=fine, in_specs=in_specs, out_specs=(P(row, col), P(row, col)), check_vma=False)
```

```python
import functools
import jax
import jax.numpy as jnp
from jax import lax
from jax.experimental import pallas as pl
from jax.experimental.pallas import tpu as pltpu
from jax.sharding import Mesh, PartitionSpec as P


HI = lax.Precision.HIGHEST
PLANE_T = ("y", "x")
GRANT = 16 * 1024 * 1024
VMEM = pl.BlockSpec(memory_space=pltpu.VMEM)


def contract(a, b, dims):
    return lax.dot_general(a, b, (dims, ((), ())), precision=HI, preferred_element_type=jnp.float32)


def mul(a, b):
    return jnp.dot(a, b, precision=HI, preferred_element_type=jnp.float32)


def share(value, axis, count):
    return lax.all_to_all(jnp.broadcast_to(value[None], (count,) + value.shape), axis, 0, 0)


def swap(value):
    return lax.ppermute(value, "k", [(0, 1), (1, 0)])


def f32(*shape):
    return jax.ShapeDtypeStruct(shape, jnp.float32)


def local(kernel, out_shape, *operands, flops=0):
    outs = out_shape if isinstance(out_shape, tuple) else (out_shape,)
    moved = sum(4 * o.size for o in operands) + sum(4 * o.size for o in outs)
    return pl.pallas_call(
        kernel,
        out_shape=out_shape,
        in_specs=[VMEM] * len(operands),
        out_specs=tuple(VMEM for _ in outs) if isinstance(out_shape, tuple) else VMEM,
        cost_estimate=pl.CostEstimate(flops=flops, bytes_accessed=moved, transcendentals=0),
        compiler_params=pltpu.CompilerParams(vmem_limit_bytes=GRANT),
    )(*operands)


def invert_kernel(own_ref, other_ref, o_ref, full):
    first = lax.axis_index("k") == 0
    u = joined(first, own_ref[...], other_ref[...])
    n = u.shape[0] // 2
    row = lax.broadcasted_iota(jnp.int32, (n, n), 0)
    col = lax.broadcasted_iota(jnp.int32, (n, n), 1)
    us = [u[:n, :n], u[n:, n:]]
    xs = [jnp.where(row == col, 1.0 / v, 0.0) for v in us]
    s = 0
    while (1 << s) < n:
        above = ((row >> (s + 1)) == (col >> (s + 1))) & (((row >> s) & 1) == 0) & (((col >> s) & 1) == 1)
        ts = [mul(x, jnp.where(above, v, 0.0)) for x, v in zip(xs, us)]
        xs = [x - mul(t, x) for x, t in zip(xs, ts)]
        s += 1
    full[:n, :n] = xs[0]
    full[n:, n:] = xs[1]
    full[:n, n:] = -mul(mul(xs[0], u[:n, n:]), xs[1])
    full[n:, :n] = jnp.zeros((n, n), jnp.float32)
    half = o_ref.shape[0]
    o_ref[...] = full[pl.ds(pl.multiple_of(lax.axis_index("k") * half, half), half), :]


def invert(own, other):
    half, n = own.shape
    return pl.pallas_call(
        invert_kernel,
        out_shape=f32(half, n),
        in_specs=[VMEM, VMEM],
        out_specs=VMEM,
        scratch_shapes=[pltpu.VMEM((n, n), jnp.float32)],
        cost_estimate=pl.CostEstimate(flops=32 * 6 * n * n * n, bytes_accessed=12 * half * n, transcendentals=0),
        compiler_params=pltpu.CompilerParams(vmem_limit_bytes=GRANT),
        name="invert_block",
    )(own, other)


def copy_kernel(a_ref, o_ref):
    o_ref[...] = a_ref[...]


def joined(first, mine, other):
    return jnp.concatenate([jnp.where(first, mine, other), jnp.where(first, other, mine)], axis=0)


def join_kernel(*refs):
    at = 0
    for ref in refs[:-1]:
        for slot in range(ref.shape[0]):
            refs[-1][at] = ref[slot]
            at += 1


def pack_kernel(own_ref, o_ref):
    for slot, block in enumerate((lax.axis_index("y"), 0, 1)):
        o_ref[slot] = own_ref[block]


def rows_kernel(own_ref, own_other_ref, mine_ref, other_ref, o_ref):
    y = lax.axis_index("y")
    first = lax.axis_index("k") == 0
    n = own_ref.shape[2]

    def block(slot):
        return joined(first, mine_ref[slot], other_ref[slot])

    diag = joined(first, own_ref[y], own_other_ref[y])
    a = mul(jnp.concatenate([joined(first, own_ref[m], own_other_ref[m]) for m in range(3)], axis=0), diag)
    zero = jnp.zeros_like(diag)
    near, far = block(0), block(3)
    y2 = jnp.where(y > 2, -mul(near, a[2 * n :]), zero)
    t1 = a[n : 2 * n] + mul(block(2), y2)
    y1 = jnp.where(y > 1, -mul(jnp.where(y > 2, far, near), t1), zero)
    t0 = a[:n] + mul(jnp.where(y > 2, block(4), block(1)), y1) + mul(block(1), y2)
    y0 = jnp.where(y > 0, -mul(jnp.where(y > 2, block(5), jnp.where(y > 1, far, near)), t0), zero)
    for m, value in enumerate((y0, y1, y2, zero)):
        o_ref[m] = jnp.where(y == m, diag, value)


def solve_kernel(j, right_ref, inv_ref, *refs):
    outs = refs[-3:] if j == 3 else refs[-2:]
    value = jnp.zeros(outs[0].shape, jnp.float32)
    for m in range(4):
        right = right_ref[m] if j == 0 else sum(right_ref[s, m] for s in range(4))
        value = value + mul(right, inv_ref[m])
    if j > 0:
        value = jnp.where(lax.axis_index("x") == j, value, refs[0][...])
    outs[0][...] = value
    for to in range(4):
        outs[1][to] = value
    if j == 3:
        outs[2][...] = value


def gram_kernel(all_ref, own_ref, o_ref):
    every = all_ref[...].reshape(-1, own_ref.shape[1])
    o_ref[...] = lax.dot_general(own_ref[...], every, (((1,), (1,)), ((), ())), precision=HI, preferred_element_type=jnp.float32)


def split_kernel(near_ref, all_ref, own_ref, o_ref):
    qc = own_ref.shape[0]
    every = all_ref[...].reshape(-1, own_ref.shape[1])
    far = lax.dot_general(own_ref[...], every, (((1,), (1,)), ((), ())), precision=HI, preferred_element_type=jnp.float32)
    near = near_ref[...]
    lane = lax.broadcasted_iota(jnp.int32, (qc, 128), 1)
    for c in range(16):
        at = c * qc // 128 * 128
        shift = c * qc % 128
        a = pltpu.roll(near[:, at : at + 128], (128 - shift) % 128, 1)
        b = pltpu.roll(far[:, at : at + 128], (128 - shift + qc) % 128, 1)
        value = jnp.where(lane < qc, a, b)
        low = pltpu.roll(value[qc // 2 :], 64, 1)
        o_ref[c] = jnp.where(lane[: qc // 2] < 2 * qc, value[: qc // 2], low)


def final_kernel(part_ref, prior_ref, query_ref, o_ref):
    total = part_ref[0]
    for s in range(1, part_ref.shape[0]):
        total = total + part_ref[s]
    total = jnp.concatenate([total, pltpu.roll(total, 64, 1)], axis=0)
    qc = total.shape[0]
    lane = lax.broadcasted_iota(jnp.int32, total.shape, 1)
    turned = jnp.where(lane < qc, pltpu.roll(total, 128 - qc, 1), pltpu.roll(total, qc, 1))
    total = jnp.where(lax.axis_index("k") == 0, total, turned)
    o_ref[...] = query_ref[...] - (prior_ref[...] + total[:, : 2 * qc])


def update_kernel(j, got_ref, panel_ref, other_ref, old_ref, new_ref, sent_ref):
    first = lax.axis_index("k") == 0
    known = got_ref[j if got_ref.shape[0] > 1 else 0]
    for m in range(4):
        old = jnp.where(lax.axis_index("y") == m, old_ref[...], 0.0) if j == 0 else old_ref[m]
        value = old - mul(known, joined(first, panel_ref[0, m], other_ref[0, m]))
        new_ref[m] = value
        for to in range(4):
            sent_ref[to, m] = value


def update(j, got, panels, others, old):
    qc, n = got.shape[1:]
    whole = lambda a: pl.BlockSpec(a.shape, lambda i: (0,) * a.ndim)
    outs = (f32(4, qc, n), f32(4, 4, qc, n))
    panel = pl.BlockSpec((1,) + panels.shape[1:], lambda i: (j, 0, 0, 0))
    in_hbm = lambda a: pltpu.with_memory_space_constraint(a, pltpu.HBM)
    return pl.pallas_call(
        functools.partial(update_kernel, j),
        out_shape=outs,
        grid=(1,),
        in_specs=[whole(got), panel, panel, whole(old)],
        out_specs=tuple(whole(o) for o in outs),
        cost_estimate=pl.CostEstimate(flops=12 * 4 * qc * n * n, bytes_accessed=4 * 4 * n * n + 24 * 4 * qc * n, transcendentals=0),
        compiler_params=pltpu.CompilerParams(vmem_limit_bytes=GRANT),
    )(got, in_hbm(panels), in_hbm(others), old)


def body(l_rows, v_prev, l_tail, k_cross, k_query):
    x_id, y_id, k_id = lax.axis_index("x"), lax.axis_index("y"), lax.axis_index("k")
    zh_id, zl_id = lax.axis_index("zh"), lax.axis_index("zl")
    rows = l_rows.shape[0]
    qc = k_cross.shape[1]

    vt = v_prev.T
    vt_other = swap(vt)
    v_pair = jnp.concatenate([vt, vt_other], axis=1)
    v_half = lax.dynamic_slice_in_dim(v_pair, k_id * qc, qc, 0)

    block = l_tail.T
    turn = [
        (((x * 4 + y) * 4 + h) * 4 + l, ((x * 4 + l) * 4 + h) * 4 + y)
        for x in range(4) for y in range(4) for h in range(4) for l in range(4) if h != x
    ]
    other = swap(block)
    turned = lax.ppermute(block, ("x", "y", "zh", "zl"), turn)
    inverted = invert(block, other)
    block = jnp.where(zh_id == x_id, jnp.where(zl_id == y_id, inverted, block), turned)
    block, v_half = lax.optimization_barrier((block, v_half))
    panels = lax.all_gather(block, ("zh", "zl"), axis=0)
    panels = panels.reshape(4, 4, rows // 2, rows)

    l_other = swap(l_rows)
    l_pair = jnp.concatenate([l_rows, l_other], axis=1)
    v_all = share(v_half, PLANE_T, 16)
    update_all = contract(v_all, l_pair, ((2,), (1,)))
    prior = contract(v_all, v_pair, ((2,), (1,)))


    prior = lax.psum_scatter(prior.reshape(16 * qc, -1), ("zl", "zh"), scatter_dimension=0, tiled=True)
    both = lax.all_to_all(update_all.reshape(4, 4, qc, rows), "zl", 0, 0)
    both = both.sum(0)
    both = lax.all_to_all(both, "zh", 0, 0)
    both = both.sum(0)
    cross = local(copy_kernel, f32(qc, rows), k_cross.T)
    rest = cross - both

    own = lax.dynamic_slice_in_dim(panels, x_id, 1, 0)[0]
    sent = local(pack_kernel, f32(3, rows // 2, rows), own)
    got = []
    for d in range(3):
        got.append(lax.ppermute(sent[: 3 - d], "y", [(y, y + 1 + d) for y in range(3 - d)]))
    mine = local(join_kernel, f32(6, rows // 2, rows), *got)
    theirs = swap(mine)
    others = swap(panels)
    own_others = lax.dynamic_slice_in_dim(others, x_id, 1, 0)[0]
    inverse = local(rows_kernel, f32(4, rows, rows), own, own_others, mine, theirs, flops=8 * 12 * rows**3)

    partial_rest = rest
    right = share(rest, "y", 4)
    solved = ()
    for j in range(4):
        solved, sent, *again = local(
            functools.partial(solve_kernel, j), (f32(qc, rows), f32(4, qc, rows)) + (f32(qc, rows),) * (j == 3),
            right, inverse, *solved, flops=12 * 4 * qc * rows * rows,
        )
        if j < 3:
            solved = (solved,)
            if j == 2:
                got = lax.ppermute(solved[0], "x", [(2, 3)])[None]
            else:
                got = lax.all_to_all(sent, "x", 0, 0)
            partial_rest, sent = update(j, got, panels, others, partial_rest)
            right = lax.all_to_all(sent, "y", 0, 0)

    near = lax.all_to_all(sent, "zh", 0, 0)
    near, prior = lax.optimization_barrier((near, prior))
    near = share(near, "zl", 4)
    far = swap(near)
    flops = 12 * 16 * qc * qc * rows
    part = local(gram_kernel, f32(qc, 16 * qc), near, again[0], flops=flops)
    part = local(split_kernel, f32(16, qc // 2, 128), part, far, again[0], flops=flops)
    part = lax.all_to_all(part, PLANE_T, 0, 0)
    posterior = local(final_kernel, f32(qc, 2 * qc), part, prior, k_query.T).T
    return solved.T, posterior


def solution(mesh):
    fine = Mesh(mesh.devices.reshape(4, 4, 4, 4, 2), ("x", "y", "zh", "zl", "k"))
    row, col = ("x", "y"), ("zh", "zl", "k")
    in_specs = (P(row, col), P(col, row), P(row, col), P(row, col), P(row, col))
    return jax.shard_map(body, mesh=fine, in_specs=in_specs, out_specs=(P(row, col), P(row, col)), check_vma=False)
```
